32 devices in a mesh: grp: 2 (over x), seq: 16 (over z, y, core).
Axes of the slice: x: 2, y: 2, z: 4, core: 2. Of those that a mesh axis runs over, the one named last changes fastest.
Arguments:
- inputs: bfloat16 [4096, 4096], P(('grp', 'seq')), parts along dimension 0, may hold values from -6 to 6
- in_weight: bfloat16 [4096, 768], replicated, may hold values from -0.09375 to 0.09375
- filter_taps: float32 [2048, 256], P('seq'), may hold values from -6 to 6
- grad_out: bfloat16 [4096, 256], P(('grp', 'seq')), parts along dimension 0, may hold values from -6 to 6
Outputs:
- grad_inputs: bfloat16 [4096, 4096], P(('grp', 'seq')), parts along dimension 0
- grad_weight: float32 [8192, 768], P(('grp', 'seq')), parts along dimension 0
- grad_taps: float32 [4096, 256], P(('grp', 'seq')), parts along dimension 0
The draws below stay inside these ranges and needn't reach their ends.
There are 2 independent parts, one for each index of `grp`. The reference program is written for one: setup_inputs(seed, part) draws one part's arguments, and reference() takes and returns one part's arrays. A program takes and returns all parts, laid end to end along the dimension named above; an argument that names none is the same for every part. Nothing has to cross between parts.
All inputs are finite; a program needn't handle non-finite values.
Results may differ from the reference program's by a relative error of at most 0.0064.
Values sent between devices are 32-bit elements; how exact they have to be, the bound alone decides.
A program may use at most 128 MiB of HBM per device.

```python
import math
import jax
import jax.numpy as jnp
from jax import lax

D = 4096
CH = 256
SEQ = 2048


def raised(result, stream_key, source, target, parts, factor):
    def block_of(axis_at):
        return (jnp.arange(result.shape[axis_at]) // (result.shape[axis_at] // parts)).reshape((-1,) + (1,) * (result.ndim - 1 - axis_at))

    first = jax.random.permutation(stream_key, parts)[block_of(target)]
    second = (block_of(target) + parts // 2) % parts
    return jnp.where((block_of(source) == first) | (block_of(source) == second), factor * result, result)


def shard_levels(stream_key, dims, cuts, smallest, high):
    gain = 1.0
    for position, parts in cuts:
        steps = jax.random.uniform(jax.random.fold_in(jax.random.fold_in(stream_key, 6), position), (parts,), jnp.float32, smallest / len(cuts), high / len(cuts))
        gain = gain * jnp.repeat(jnp.exp(steps), dims[position] // parts).reshape((-1,) + (1,) * (len(dims) - 1 - position))
    return gain


def normal_values(own_key, shape, width, limit, split=(), kind=jnp.bfloat16):
    level = shard_levels(own_key, shape, split, -0.22, 0.18) if split else 1.0
    drawn = jax.random.normal(own_key, shape, jnp.float32) * width * level
    return jnp.minimum(jnp.maximum(drawn, -limit), limit).astype(kind)


def heavy_noise(own_key, shape, spread, bound, split, heavy, kind=jnp.bfloat16):
    drawn = spread * jax.random.normal(own_key, shape, jnp.float32)
    if split:
        drawn = drawn * shard_levels(own_key, shape, split, -0.22, 0.18)
    return jnp.clip(raised(drawn, jax.random.fold_in(own_key, 3), *heavy), -bound, bound).astype(kind)


def setup_inputs(seed: int = 0, part: int = 0) -> dict:
    seeds = jax.random.split(jax.random.key(seed), 5)
    part_keys = jax.random.split(jax.random.fold_in(seeds[4], part), 5)
    inputs = heavy_noise(part_keys[0], (SEQ, D), 1.0, 6.0, ((0, 16),), (0, 1, 16, 2.0))
    in_weight = normal_values(seeds[1], (D, 3 * CH), D ** -0.5, 0.09375)
    filter_taps = normal_values(seeds[2], (SEQ, CH), 1.0, 6.0, ((0, 16),), jnp.float32)
    grad_out = normal_values(part_keys[3], (SEQ, CH), 1.0, 6.0, ((0, 16),))
    return {"inputs": inputs, "in_weight": in_weight, "filter_taps": filter_taps, "grad_out": grad_out}


def reference(inputs, in_weight, filter_taps, grad_out):
    seqlen = inputs.shape[0]
    channels = filter_taps.shape[1]
    scaling = 1.0 / math.sqrt(seqlen)
    projected = jnp.dot(inputs, in_weight, preferred_element_type=jnp.float32).astype(jnp.bfloat16)
    query_rows = projected[:, :channels].astype(jnp.float32)
    key_rows = projected[:, channels:2 * channels].astype(jnp.float32)
    value_rows = projected[:, 2 * channels:].astype(jnp.float32)
    gated_input = key_rows * value_rows
    kernel = filter_taps * scaling
    back_grad = grad_out.astype(jnp.float32) * query_rows
    fft_length = 2 * seqlen
    kernel_spec = jnp.fft.rfft(kernel, n=fft_length, axis=0)
    gated_spec = jnp.fft.rfft(gated_input, n=fft_length, axis=0)
    back_spec = jnp.fft.rfft(back_grad, n=fft_length, axis=0)
    mixed_rows = jnp.fft.irfft(kernel_spec * gated_spec, n=fft_length, axis=0)[:seqlen]
    back_conv = jnp.fft.irfft(jnp.conj(kernel_spec) * back_spec, n=fft_length, axis=0)[:seqlen]
    grad_taps = jnp.fft.irfft(back_spec * jnp.conj(gated_spec), n=fft_length, axis=0)[:seqlen] * scaling
    grad_proj = jnp.concatenate([grad_out.astype(jnp.float32) * mixed_rows, back_conv * value_rows, back_conv * key_rows], axis=1).astype(jnp.bfloat16)
    grad_inputs = lax.dot_general(grad_proj, in_weight, (((1,), (1,)), ((), ())), preferred_element_type=jnp.float32).astype(jnp.bfloat16)
    grad_weight = lax.dot_general(inputs, grad_proj, (((0,), (0,)), ((), ())), preferred_element_type=jnp.float32) * scaling
    return (grad_inputs, grad_weight, grad_taps.astype(jnp.float32))
```

```python
import functools
import math

import jax
import jax.numpy as jnp
from jax import lax
from jax.experimental import pallas as pl
from jax.experimental.pallas import tpu as pltpu
from jax.sharding import PartitionSpec as P

GROUP = 16


def round_up(value, step):
    return (value + step - 1) // step * step


def remote(src, dst, send_sem, recv_sem, peer):
    return pltpu.make_async_remote_copy(
        src_ref=src,
        dst_ref=dst,
        send_sem=send_sem,
        recv_sem=recv_sem,
        device_id={"seq": peer},
        device_id_type=pl.DeviceIdType.MESH,
    )


def conv_kernel(
    n, cpd, wide, slim, pairs_ref, back_ref, mixed_ref, rest_ref,
    got_pairs, got_back, made_mixed, made_rest, pad_gated, pad_back,
    send_sems, recv_sems, send_back_sems, recv_back_sems,
):
    me = lax.axis_index("seq")
    rows = pairs_ref.shape[1]

    def slot(ref, index, height):
        return ref.at[pl.ds(pl.multiple_of(index * height, 8), height), :]

    barrier = pltpu.get_barrier_semaphore()

    @pl.loop(1, n)
    def _(o):
        pl.semaphore_signal(
            barrier, inc=1, device_id={"seq": lax.rem(me + o, n)},
            device_id_type=pl.DeviceIdType.MESH,
        )

    pl.semaphore_wait(barrier, n - 1)

    def forth(peer, sender):
        return (
            remote(slot(pairs_ref, peer, wide), slot(got_pairs, sender, wide),
                   send_sems.at[0, peer], recv_sems.at[0, sender], peer),
            remote(slot(back_ref, peer, slim), slot(got_back, n - 1 - sender, slim),
                   send_sems.at[1, peer], recv_sems.at[1, sender], peer),
        )

    def home(peer, sender):
        return (
            remote(slot(made_mixed, peer, slim), slot(mixed_ref, sender, slim),
                   send_back_sems.at[0, peer], recv_back_sems.at[0, sender], peer),
            remote(slot(made_rest, n - 1 - peer, wide), slot(rest_ref, sender, wide),
                   send_back_sems.at[1, peer], recv_back_sems.at[1, sender], peer),
        )

    def exchange_start(plan):
        @pl.loop(1, n)
        def _(o):
            for copy in plan(lax.rem(me + o, n), me):
                copy.start()

    def exchange_wait(plan):
        @pl.loop(1, n)
        def _(o):
            other = lax.rem(me + n - o, n)
            for copy in plan(other, other):
                copy.wait_recv()

    def exchange_sent(plan):
        @pl.loop(1, n)
        def _(o):
            for copy in plan(lax.rem(me + o, n), me):
                copy.wait_send()

    exchange_start(forth)
    slot(got_pairs, me, wide)[...] = slot(pairs_ref, me, wide)[...]
    slot(got_back, n - 1 - me, slim)[...] = slot(back_ref, me, slim)[...]
    pad_gated[pl.ds(0, n), :] = jnp.zeros((n, rows), jnp.float32)
    pad_back[pl.ds(0, n), :] = jnp.zeros((n, rows), jnp.float32)
    exchange_wait(forth)

    lane = lax.broadcasted_iota(jnp.int32, (rows, rows), 1)
    line = lax.broadcasted_iota(jnp.int32, (rows, rows), 0)
    keep = lane >= line
    group = min(GROUP, n)

    def turned(first, index):
        block = got_pairs[pl.ds(index * wide + first, 1), :]
        return pltpu.roll(
            jnp.broadcast_to(block, (rows, rows)), 0, 1, stride=1, stride_axis=0
        )

    def channel(c, carry):
        pad_gated[pl.ds(n, n), :] = got_pairs[pl.ds(cpd + c, n, stride=wide), :]
        pad_back[pl.ds(n, n), :] = got_back[pl.ds(c, n, stride=slim), :]

        def some_lags(q, total):
            matrices = []
            for first in (c, cpd + c):
                if isinstance(q, int):
                    before = jnp.zeros((rows, rows), jnp.float32)
                else:
                    before = turned(first, jnp.maximum(q * group - 1, 0))
                    before = jnp.where(q == 0, 0.0, before)
                parts = []
                for e in range(group):
                    now = turned(first, q * group + e)
                    parts.append(jnp.where(keep, now, before).astype(jnp.bfloat16))
                    before = now
                matrices.append(jnp.concatenate(parts, axis=0))
            table = jnp.concatenate(matrices, axis=1)
            left = jnp.concatenate(
                [
                    jnp.concatenate(
                        [pad[pl.ds(n - q * group - e, n), :] for e in range(group)], axis=1
                    ).astype(jnp.bfloat16)
                    for pad in (pad_gated, pad_back)
                ],
                axis=0,
            )
            return total + jnp.dot(left, table, preferred_element_type=jnp.float32)

        total = jnp.zeros((2 * n, 2 * rows), jnp.float32)
        if n == group:
            total = some_lags(0, total)
        else:
            total = lax.fori_loop(0, n // group, some_lags, total)
        made_mixed[pl.ds(c, n, stride=slim), :] = total[:n, :rows]
        made_rest[pl.ds(c, n, stride=wide), :] = total[n:, :rows]
        made_rest[pl.ds(cpd + c, n, stride=wide), :] = total[n:, rows:]
        return carry

    lax.fori_loop(0, cpd, channel, 0)
    exchange_sent(forth)
    exchange_start(home)
    slot(mixed_ref, me, slim)[...] = slot(made_mixed, me, slim)[...]
    slot(rest_ref, me, wide)[...] = slot(made_rest, n - 1 - me, wide)[...]
    exchange_wait(home)
    exchange_sent(home)


def convolve(filter_taps, gated_input, back_grad, n):
    rows, channels = filter_taps.shape
    cpd = channels // n
    wide, slim = round_up(2 * cpd, 8), round_up(cpd, 8)

    def by_owner(signals, height):
        stacked = jnp.stack([s.T.reshape(n, cpd, rows) for s in signals], axis=1)
        stacked = stacked.reshape(n, len(signals) * cpd, rows)
        stacked = jnp.pad(stacked, ((0, 0), (0, height - stacked.shape[1]), (0, 0)))
        return stacked.reshape(n * height, rows)

    def to_rows(blocks, height, count):
        shaped = blocks.reshape(n, height, rows)[:, : count * cpd].reshape(n, count, cpd, rows)
        return [shaped[:, k].reshape(channels, rows).T for k in range(count)]

    vmem = pl.BlockSpec(memory_space=pltpu.VMEM)
    f32 = jnp.float32
    mixed, rest = pl.pallas_call(
        functools.partial(conv_kernel, n, cpd, wide, slim),
        out_shape=(
            jax.ShapeDtypeStruct((n * slim, rows), f32),
            jax.ShapeDtypeStruct((n * wide, rows), f32),
        ),
        in_specs=[vmem, vmem],
        out_specs=(vmem, vmem),
        scratch_shapes=[
            pltpu.VMEM((n * wide, rows), f32),
            pltpu.VMEM((n * slim, rows), f32),
            pltpu.VMEM((n * slim, rows), f32),
            pltpu.VMEM((n * wide, rows), f32),
            pltpu.VMEM((2 * n, rows), f32),
            pltpu.VMEM((2 * n, rows), f32),
            pltpu.SemaphoreType.DMA((2, n)),
            pltpu.SemaphoreType.DMA((2, n)),
            pltpu.SemaphoreType.DMA((2, n)),
            pltpu.SemaphoreType.DMA((2, n)),
        ],
        compiler_params=pltpu.CompilerParams(collective_id=0, has_side_effects=True),
    )(
        by_owner([filter_taps, gated_input], wide),
        by_owner([jnp.flip(back_grad, axis=0)], slim),
    )
    (mixed_rows,) = to_rows(mixed, slim, 1)
    back_conv, grad_taps = to_rows(rest, wide, 2)
    return mixed_rows, jnp.flip(back_conv, axis=0), jnp.flip(grad_taps, axis=0)


def per_device(inputs, in_weight, filter_taps, grad_out):
    row_count = inputs.shape[0]
    channels = filter_taps.shape[1]
    seq_count = lax.axis_size("seq")
    seqlen = row_count * seq_count
    scaling = 1.0 / math.sqrt(seqlen)
    projected = jnp.dot(inputs, in_weight, preferred_element_type=jnp.float32).astype(jnp.bfloat16)
    query_rows = projected[:, :channels].astype(jnp.float32)
    key_rows = projected[:, channels : 2 * channels].astype(jnp.float32)
    value_rows = projected[:, 2 * channels :].astype(jnp.float32)
    gated_input = key_rows * value_rows
    back_grad = grad_out.astype(jnp.float32) * query_rows
    mixed_rows, back_conv, grad_taps = convolve(filter_taps, gated_input, back_grad, seq_count)
    mixed_rows = mixed_rows * scaling
    back_conv = back_conv * scaling
    grad_taps = grad_taps * scaling
    grad_proj = jnp.concatenate(
        [grad_out.astype(jnp.float32) * mixed_rows, back_conv * value_rows, back_conv * key_rows],
        axis=1,
    ).astype(jnp.bfloat16)
    grad_inputs = lax.dot_general(
        grad_proj, in_weight, (((1,), (1,)), ((), ())), preferred_element_type=jnp.float32
    ).astype(jnp.bfloat16)
    grad_weight = lax.psum_scatter(
        lax.dot_general(
            inputs, grad_proj, (((0,), (0,)), ((), ())), preferred_element_type=jnp.float32
        )
        * scaling,
        "seq",
        scatter_dimension=0,
        tiled=True,
    )
    return (grad_inputs, grad_weight, grad_taps)


def solution(mesh):
    in_specs = (P(("grp", "seq"), None), P(), P("seq", None), P(("grp", "seq"), None))
    out_specs = (P(("grp", "seq"), None), P(("grp", "seq"), None), P(("grp", "seq"), None))
    return jax.shard_map(
        per_device, mesh=mesh, in_specs=in_specs, out_specs=out_specs, check_vma=False
    )
```

```python
import functools
import math

import jax
import jax.numpy as jnp
from jax import lax
from jax.experimental import pallas as pl
from jax.experimental.pallas import tpu as pltpu
from jax.sharding import PartitionSpec as P

GROUP = 16
TEAM = 8
CHIPS = 4
PARTS = 3


def round_up(value, step):
    return (value + step - 1) // step * step


def remote(src, dst, send_sem, recv_sem, peer):
    return pltpu.make_async_remote_copy(
        src_ref=src,
        dst_ref=dst,
        send_sem=send_sem,
        recv_sem=recv_sem,
        device_id={"seq": peer},
        device_id_type=pl.DeviceIdType.MESH,
    )


def conv_kernel(
    n, cpd, wide, slim, pairs_ref, back_ref, cols_ref, mixed_ref, rest_ref, got_cols,
    got_pairs, got_back, made_mixed, made_rest, pad_gated, pad_back,
    send_sems, recv_sems, send_back_sems, recv_back_sems, send_cols_sems, recv_cols_sems,
):
    me = lax.axis_index("seq")
    rows = pairs_ref.shape[1]
    team = cols_ref.shape[0] // TEAM
    base, mine = me // TEAM * TEAM, lax.rem(me, TEAM)

    def slot(ref, index, height):
        return ref.at[pl.ds(pl.multiple_of(index * height, 8), height), :]

    barrier = pltpu.get_barrier_semaphore()

    @pl.loop(1, n)
    def _(o):
        pl.semaphore_signal(
            barrier, inc=1, device_id={"seq": lax.rem(me + o, n)},
            device_id_type=pl.DeviceIdType.MESH,
        )

    pl.semaphore_wait(barrier, n - 1)

    def forth(peer, sender):
        return (
            remote(slot(pairs_ref, peer, wide), slot(got_pairs, sender, wide),
                   send_sems.at[0, peer], recv_sems.at[0, sender], peer),
            remote(slot(back_ref, peer, slim), slot(got_back, n - 1 - sender, slim),
                   send_sems.at[1, peer], recv_sems.at[1, sender], peer),
        )

    def home(peer, sender):
        return (
            remote(slot(made_mixed, peer, slim), slot(mixed_ref, sender, slim),
                   send_back_sems.at[0, peer], recv_back_sems.at[0, sender], peer),
            remote(slot(made_rest, n - 1 - peer, wide), slot(rest_ref, sender, wide),
                   send_back_sems.at[1, peer], recv_back_sems.at[1, sender], peer),
        )

    def exchange_start(plan):
        @pl.loop(1, n)
        def _(o):
            for copy in plan(lax.rem(me + o, n), me):
                copy.start()

    def exchange_wait(plan):
        @pl.loop(1, n)
        def _(o):
            other = lax.rem(me + n - o, n)
            for copy in plan(other, other):
                copy.wait_recv()

    def exchange_sent(plan):
        @pl.loop(1, n)
        def _(o):
            for copy in plan(lax.rem(me + o, n), me):
                copy.wait_send()

    def cols(target, sender, peer):
        return remote(slot(cols_ref, target, team), slot(got_cols, sender, team),
                      send_cols_sems.at[target], recv_cols_sems.at[sender], base + peer)

    exchange_start(forth)

    @pl.loop(1, TEAM)
    def _(o):
        other = lax.rem(mine + o, TEAM)
        cols(other, mine, other).start()

    slot(got_cols, mine, team)[...] = slot(cols_ref, mine, team)[...]
    slot(got_pairs, me, wide)[...] = slot(pairs_ref, me, wide)[...]
    slot(got_back, n - 1 - me, slim)[...] = slot(back_ref, me, slim)[...]
    pad_gated[pl.ds(0, n), :] = jnp.zeros((n, rows), jnp.float32)
    pad_back[pl.ds(0, n), :] = jnp.zeros((n, rows), jnp.float32)
    exchange_wait(forth)

    lane = lax.broadcasted_iota(jnp.int32, (rows, rows), 1)
    line = lax.broadcasted_iota(jnp.int32, (rows, rows), 0)
    keep = lane >= line
    group = min(GROUP, n)

    def turned(first, index):
        block = got_pairs[pl.ds(index * wide + first, 1), :]
        return pltpu.roll(
            jnp.broadcast_to(block, (rows, rows)), 0, 1, stride=1, stride_axis=0
        )

    def channel(c, carry):
        pad_gated[pl.ds(n, n), :] = got_pairs[pl.ds(cpd + c, n, stride=wide), :]
        pad_back[pl.ds(n, n), :] = got_back[pl.ds(c, n, stride=slim), :]

        def some_lags(q, total):
            matrices = []
            for first in (c, cpd + c):
                if isinstance(q, int):
                    before = jnp.zeros((rows, rows), jnp.float32)
                else:
                    before = turned(first, jnp.maximum(q * group - 1, 0))
                    before = jnp.where(q == 0, 0.0, before)
                parts = []
                for e in range(group):
                    now = turned(first, q * group + e)
                    parts.append(jnp.where(keep, now, before).astype(jnp.bfloat16))
                    before = now
                matrices.append(jnp.concatenate(parts, axis=0))
            table = jnp.concatenate(matrices, axis=1)
            left = jnp.concatenate(
                [
                    jnp.concatenate(
                        [pad[pl.ds(n - q * group - e, n), :] for e in range(group)], axis=1
                    ).astype(jnp.bfloat16)
                    for pad in (pad_gated, pad_back)
                ],
                axis=0,
            )
            return total + jnp.dot(left, table, preferred_element_type=jnp.float32)

        total = jnp.zeros((2 * n, 2 * rows), jnp.float32)
        if n == group:
            total = some_lags(0, total)
        else:
            total = lax.fori_loop(0, n // group, some_lags, total)
        made_mixed[pl.ds(c, n, stride=slim), :] = total[:n, :rows]
        made_rest[pl.ds(c, n, stride=wide), :] = total[n:, :rows]
        made_rest[pl.ds(cpd + c, n, stride=wide), :] = total[n:, rows:]
        return carry

    lax.fori_loop(0, cpd, channel, 0)
    exchange_sent(forth)
    exchange_start(home)
    slot(mixed_ref, me, slim)[...] = slot(made_mixed, me, slim)[...]
    slot(rest_ref, me, wide)[...] = slot(made_rest, n - 1 - me, wide)[...]
    exchange_wait(home)
    exchange_sent(home)

    @pl.loop(1, TEAM)
    def _(o):
        other = lax.rem(mine + o, TEAM)
        cols(other, mine, other).wait_send()
        cols(other, other, other).wait_recv()


def convolve(filter_taps, gated_input, back_grad, columns, n):
    rows, channels = filter_taps.shape
    cpd = channels // n
    wide, slim = round_up(2 * cpd, 8), round_up(cpd, 8)

    def by_owner(signals, height):
        stacked = jnp.stack([s.T.reshape(n, cpd, rows) for s in signals], axis=1)
        stacked = stacked.reshape(n, len(signals) * cpd, rows)
        stacked = jnp.pad(stacked, ((0, 0), (0, height - stacked.shape[1]), (0, 0)))
        return stacked.reshape(n * height, rows)

    def to_rows(blocks, height, count):
        shaped = blocks.reshape(n, height, rows)[:, : count * cpd].reshape(n, count, cpd, rows)
        return [shaped[:, k].reshape(channels, rows).T for k in range(count)]

    vmem = pl.BlockSpec(memory_space=pltpu.VMEM)
    f32 = jnp.float32
    mixed, rest, got_cols = pl.pallas_call(
        functools.partial(conv_kernel, n, cpd, wide, slim),
        out_shape=(
            jax.ShapeDtypeStruct((n * slim, rows), f32),
            jax.ShapeDtypeStruct((n * wide, rows), f32),
            jax.ShapeDtypeStruct(columns.shape, f32),
        ),
        in_specs=[vmem] * 3,
        out_specs=(vmem,) * 3,
        scratch_shapes=[
            pltpu.VMEM((n * wide, rows), f32),
            pltpu.VMEM((n * slim, rows), f32),
            pltpu.VMEM((n * slim, rows), f32),
            pltpu.VMEM((n * wide, rows), f32),
            pltpu.VMEM((2 * n, rows), f32),
            pltpu.VMEM((2 * n, rows), f32),
            pltpu.SemaphoreType.DMA((2, n)),
            pltpu.SemaphoreType.DMA((2, n)),
            pltpu.SemaphoreType.DMA((2, n)),
            pltpu.SemaphoreType.DMA((2, n)),
            pltpu.SemaphoreType.DMA((TEAM,)),
            pltpu.SemaphoreType.DMA((TEAM,)),
        ],
        compiler_params=pltpu.CompilerParams(collective_id=0, has_side_effects=True),
    )(
        by_owner([filter_taps, gated_input], wide),
        by_owner([jnp.flip(back_grad, axis=0)], slim),
        columns,
    )
    (mixed_rows,) = to_rows(mixed, slim, 1)
    back_conv, grad_taps = to_rows(rest, wide, 2)
    return mixed_rows, jnp.flip(back_conv, axis=0), jnp.flip(grad_taps, axis=0), got_cols


def weight_kernel(
    n, scaling, cols_ref, proj_ref, weight_ref, grad_inputs_ref, out_ref,
    left, proj_all, made, got, weights,
    send_sems, relay_sems, recv_sems, send_sum_sems, recv_sum_sems, weight_sem,
):
    me = lax.axis_index("seq")
    teams = n // TEAM
    team, mine = me // TEAM, lax.rem(me, TEAM)
    base, chip, core = team * TEAM, mine // 2, lax.rem(mine, 2)
    sibling = chip * 2 + 1 - core
    depth = cols_ref.shape[0] // TEAM
    rows, width = proj_ref.shape[0] // PARTS, proj_ref.shape[1]
    block = depth // teams

    load = pltpu.make_async_copy(weight_ref, weights, weight_sem)
    load.start()
    barrier = pltpu.get_barrier_semaphore()

    def greet(device):
        pl.semaphore_signal(
            barrier, inc=1, device_id={"seq": device}, device_id_type=pl.DeviceIdType.MESH
        )

    @pl.loop(1, TEAM)
    def _(o):
        greet(base + lax.rem(mine + o, TEAM))

    @pl.loop(1, teams)
    def _(o):
        greet(lax.rem(team + o, teams) * TEAM + mine)

    pl.semaphore_wait(barrier, TEAM - 1 + teams - 1)

    def held(part, member):
        return proj_all.at[pl.ds(pl.multiple_of((part * TEAM + member) * rows, 8), rows), :]

    def own(part):
        return proj_ref.at[pl.ds(part * rows, rows), :]

    def direct(part, o, sender, peer):
        return remote(own(part), held(part, sender), send_sems.at[part, o],
                      recv_sems.at[part, sender], base + peer)

    def relay(part, o, member):
        return remote(held(part, member), held(part, member), relay_sems.at[part, o],
                      recv_sems.at[part, member], base + sibling)

    def across(o):
        return lax.rem(chip + o, CHIPS) * 2 + core

    def sums(part, to_team, from_team, peer):
        def place(ref, index):
            start = pl.multiple_of((part * teams + index) * block, 8)
            return ref.at[pl.ds(start, block), :]

        return remote(place(made, to_team), place(got, from_team),
                      send_sum_sems.at[part, to_team], recv_sum_sems.at[part, from_team],
                      peer * TEAM + mine)

    for part in range(PARTS):
        for o in range(1, CHIPS):
            direct(part, o, mine, across(o)).start()
        direct(part, 0, mine, sibling).start()
        held(part, mine)[...] = own(part)[...]

    for s in range(TEAM):
        left[:, s * rows : (s + 1) * rows] = cols_ref[s * depth : (s + 1) * depth, :].astype(
            jnp.bfloat16
        )
    load.wait()
    proj = jnp.concatenate(
        [own(part)[...].astype(jnp.bfloat16) for part in range(PARTS)], axis=1
    )
    tile = min(512, weights.shape[0])

    @pl.loop(0, weights.shape[0] // tile)
    def _(t):
        start = pl.multiple_of(t * tile, tile)
        grad_inputs_ref[:, pl.ds(start, tile)] = lax.dot_general(
            proj, weights[pl.ds(start, tile), :], (((1,), (1,)), ((), ())),
            preferred_element_type=jnp.float32,
        ).astype(jnp.bfloat16)

    for part in range(PARTS):
        for o in range(1, CHIPS):
            direct(part, o, across(o), across(o)).wait_recv()
            relay(part, o, across(o)).start()
        direct(part, 0, sibling, sibling).wait_recv()
        for o in range(1, CHIPS):
            relay(part, o, lax.rem(chip + o, CHIPS) * 2 + 1 - core).wait_recv()
        right = proj_all[part * TEAM * rows : (part + 1) * TEAM * rows, :].astype(jnp.bfloat16)

        def product(index):
            lines = left[pl.ds(pl.multiple_of(index * block, 16), block), :]
            return jnp.dot(lines, right, preferred_element_type=jnp.float32)

        def send_one(o, carry):
            target = lax.rem(team + o, teams)
            made[pl.ds(pl.multiple_of((part * teams + target) * block, 8), block), :] = product(
                target
            )
            sums(part, target, team, target).start()
            return carry

        lax.fori_loop(1, teams, send_one, 0)
        out_ref[:, part * width : (part + 1) * width] = product(team)

    for part in range(PARTS):
        span = slice(part * width, (part + 1) * width)

        def add_one(o, carry):
            other = lax.rem(team + o, teams)
            sums(part, other, other, other).wait_recv()
            start = pl.multiple_of((part * teams + other) * block, 8)
            out_ref[:, span] = out_ref[:, span] + got[pl.ds(start, block), :]
            return carry

        lax.fori_loop(1, teams, add_one, 0)
        out_ref[:, span] = out_ref[:, span] * scaling

    for part in range(PARTS):
        for o in range(1, CHIPS):
            direct(part, o, mine, across(o)).wait_send()
            relay(part, o, across(o)).wait_send()
        direct(part, 0, mine, sibling).wait_send()

        def sent_one(o, carry):
            target = lax.rem(team + o, teams)
            sums(part, target, team, target).wait_send()
            return carry

        lax.fori_loop(1, teams, sent_one, 0)


def weight_step(columns, proj, in_weight, scaling, n):
    depth, rows = columns.shape[0] // TEAM, columns.shape[1]
    width = proj.shape[1]
    block = in_weight.shape[0] // n
    f32 = jnp.float32
    vmem = pl.BlockSpec(memory_space=pltpu.VMEM)
    return pl.pallas_call(
        functools.partial(weight_kernel, n, scaling),
        out_shape=(
            jax.ShapeDtypeStruct((rows, in_weight.shape[0]), jnp.bfloat16),
            jax.ShapeDtypeStruct((block, PARTS * width), f32),
        ),
        in_specs=[vmem, vmem, pl.BlockSpec(memory_space=pl.ANY)],
        out_specs=(vmem, vmem),
        scratch_shapes=[
            pltpu.VMEM((depth, TEAM * rows), jnp.bfloat16),
            pltpu.VMEM((PARTS * TEAM * rows, width), f32),
            pltpu.VMEM((PARTS * depth, width), f32),
            pltpu.VMEM((PARTS * depth, width), f32),
            pltpu.VMEM(in_weight.shape, in_weight.dtype),
            pltpu.SemaphoreType.DMA((PARTS, CHIPS)),
            pltpu.SemaphoreType.DMA((PARTS, CHIPS)),
            pltpu.SemaphoreType.DMA((PARTS, TEAM)),
            pltpu.SemaphoreType.DMA((PARTS, n // TEAM)),
            pltpu.SemaphoreType.DMA((PARTS, n // TEAM)),
            pltpu.SemaphoreType.DMA,
        ],
        compiler_params=pltpu.CompilerParams(collective_id=1, has_side_effects=True),
    )(columns, proj, in_weight)


def per_device(inputs, in_weight, filter_taps, grad_out):
    row_count, depth = inputs.shape
    channels = filter_taps.shape[1]
    seq_count = lax.axis_size("seq")
    seqlen = row_count * seq_count
    scaling = 1.0 / math.sqrt(seqlen)
    columns = inputs.T.reshape(seq_count // TEAM, TEAM, depth // seq_count, row_count)
    columns = columns.transpose(1, 0, 2, 3).reshape(depth, row_count).astype(jnp.float32)
    projected = jnp.dot(inputs, in_weight, preferred_element_type=jnp.float32).astype(jnp.bfloat16)
    query_rows = projected[:, :channels].astype(jnp.float32)
    key_rows = projected[:, channels : 2 * channels].astype(jnp.float32)
    value_rows = projected[:, 2 * channels :].astype(jnp.float32)
    gated_input = key_rows * value_rows
    back_grad = grad_out.astype(jnp.float32) * query_rows
    mixed_rows, back_conv, grad_taps, got_cols = convolve(
        filter_taps, gated_input, back_grad, columns, seq_count
    )
    mixed_rows = mixed_rows * scaling
    back_conv = back_conv * scaling
    grad_taps = grad_taps * scaling
    grad_proj = jnp.concatenate(
        [grad_out.astype(jnp.float32) * mixed_rows, back_conv * value_rows, back_conv * key_rows],
        axis=0,
    )
    grad_inputs, grad_weight = weight_step(got_cols, grad_proj, in_weight, scaling, seq_count)
    return (grad_inputs, grad_weight, grad_taps)


def solution(mesh):
    in_specs = (P(("grp", "seq"), None), P(), P("seq", None), P(("grp", "seq"), None))
    out_specs = (P(("grp", "seq"), None), P(("grp", "seq"), None), P(("grp", "seq"), None))
    return jax.shard_map(
        per_device, mesh=mesh, in_specs=in_specs, out_specs=out_specs, check_vma=False
    )
```

```python
import functools
import math

import jax
import jax.numpy as jnp
from jax import lax
from jax.experimental import pallas as pl
from jax.experimental.pallas import tpu as pltpu
from jax.sharding import PartitionSpec as P

GROUP = 16
TEAM = 8
CHIPS = 4
PARTS = 3


def round_up(value, step):
    return (value + step - 1) // step * step


def remote(src, dst, send_sem, recv_sem, peer):
    return pltpu.make_async_remote_copy(
        src_ref=src,
        dst_ref=dst,
        send_sem=send_sem,
        recv_sem=recv_sem,
        device_id={"seq": peer},
        device_id_type=pl.DeviceIdType.MESH,
    )


def fused_kernel(
    n, scaling, x_ref, weight_ref, taps_ref, grad_ref,
    grad_inputs_ref, out_ref, grad_taps_ref,
    send_taps, send_gated, send_back, got_taps, got_gated, got_back,
    made_mixed, made_conv, made_taps, home_mixed, home_conv, home_taps,
    pad_gated, pad_back, send_cols, got_cols, left, key_rows, value_rows,
    proj, proj_all, made, got, weights,
    go_sems, come_sems, back_sems, home_sems, send_cols_sems, recv_cols_sems,
    send_sems, relay_sems, recv_sems, send_sum_sems, recv_sum_sems, weight_sems,
):
    f32, bf16 = jnp.float32, jnp.bfloat16
    me = lax.axis_index("seq")
    rows, depth = x_ref.shape
    channels = taps_ref.shape[1]
    cpd = channels // n
    slim = send_taps.shape[0] // n
    teams = n // TEAM
    team, mine = me // TEAM, lax.rem(me, TEAM)
    base, chip, core = team * TEAM, mine // 2, lax.rem(mine, 2)
    sibling = chip * 2 + 1 - core
    block = depth // n
    share = depth // TEAM
    pieces = weight_sems.shape[0]
    piece = depth // pieces

    def slot(ref, index, height):
        return ref.at[pl.ds(pl.multiple_of(index * height, 8), height), :]

    def load(k):
        span = pl.ds(k * piece, piece)
        return pltpu.make_async_copy(
            weight_ref.at[span, :], weights.at[span, :], weight_sems.at[k]
        )

    for k in range(pieces):
        load(k).start()
    barrier = pltpu.get_barrier_semaphore()

    @pl.loop(1, n)
    def _(o):
        pl.semaphore_signal(
            barrier, inc=1, device_id={"seq": lax.rem(me + o, n)},
            device_id_type=pl.DeviceIdType.MESH,
        )

    def spread(ref, values):
        if slim == cpd:
            ref[...] = values
        else:
            for p in range(n):
                ref[p * slim : p * slim + cpd, :] = values[p * cpd : (p + 1) * cpd, :]

    def gather(ref):
        if slim == cpd:
            return ref[...]
        return jnp.concatenate([ref[p * slim : p * slim + cpd, :] for p in range(n)], axis=0)

    anti = (
        lax.broadcasted_iota(jnp.int32, (rows, rows), 0)
        + lax.broadcasted_iota(jnp.int32, (rows, rows), 1)
        == rows - 1
    ).astype(f32)

    def reverse(values):
        return jnp.dot(
            values, anti, preferred_element_type=f32, precision=lax.Precision.HIGHEST
        )

    spread(send_taps, taps_ref[...].T)
    for g in range(TEAM):
        for h in range(teams):
            first = (h * TEAM + g) * block
            send_cols[g * rows : (g + 1) * rows, h * block : (h + 1) * block] = x_ref[
                :, first : first + block
            ].astype(f32)
    pl.semaphore_wait(barrier, n - 1)

    def forth_taps(peer, sender):
        return (remote(slot(send_taps, peer, slim), slot(got_taps, sender, slim),
                       go_sems.at[0, peer], come_sems.at[0, sender], peer),)

    def forth(peer, sender):
        return (
            remote(slot(send_gated, peer, slim), slot(got_gated, sender, slim),
                   go_sems.at[1, peer], come_sems.at[1, sender], peer),
            remote(slot(send_back, peer, slim), slot(got_back, n - 1 - sender, slim),
                   go_sems.at[2, peer], come_sems.at[2, sender], peer),
        )

    def home(peer, sender):
        return (
            remote(slot(made_mixed, peer, slim), slot(home_mixed, sender, slim),
                   back_sems.at[0, peer], home_sems.at[0, sender], peer),
            remote(slot(made_conv, n - 1 - peer, slim), slot(home_conv, sender, slim),
                   back_sems.at[1, peer], home_sems.at[1, sender], peer),
        )

    def home_last(peer, sender):
        return (remote(slot(made_taps, n - 1 - peer, slim), slot(home_taps, sender, slim),
                       back_sems.at[2, peer], home_sems.at[2, sender], peer),)

    def exchange_start(plan):
        @pl.loop(1, n)
        def _(o):
            for copy in plan(lax.rem(me + o, n), me):
                copy.start()

    def exchange_wait(plan):
        @pl.loop(1, n)
        def _(o):
            other = lax.rem(me + n - o, n)
            for copy in plan(other, other):
                copy.wait_recv()

    def exchange_sent(plan):
        @pl.loop(1, n)
        def _(o):
            for copy in plan(lax.rem(me + o, n), me):
                copy.wait_send()

    def cols(target, sender, peer):
        return remote(slot(send_cols, target, rows), slot(got_cols, sender, rows),
                      send_cols_sems.at[target], recv_cols_sems.at[sender], base + peer)

    def cols_start(other):
        cols(other, mine, other).start()

    exchange_start(forth_taps)
    cols_start(sibling)
    total = jnp.zeros((rows, PARTS * channels), f32)
    for k in range(pieces):
        load(k).wait()
        total = total + jnp.dot(
            x_ref[:, k * piece : (k + 1) * piece], weights[k * piece : (k + 1) * piece, :],
            preferred_element_type=f32,
        )
    total = total.astype(bf16).astype(f32)
    key_rows[...] = total[:, channels : 2 * channels]
    value_rows[...] = total[:, 2 * channels :]
    spread(send_gated, (total[:, channels : 2 * channels] * total[:, 2 * channels :]).T)
    spread(send_back, reverse((grad_ref[...].astype(f32) * total[:, :channels]).T))
    exchange_start(forth)
    for o in range(1, CHIPS):
        cols_start(lax.rem(chip + o, CHIPS) * 2 + core)
        cols_start(lax.rem(chip + o, CHIPS) * 2 + 1 - core)

    slot(got_cols, mine, rows)[...] = slot(send_cols, mine, rows)[...]
    slot(got_taps, me, slim)[...] = slot(send_taps, me, slim)[...]
    slot(got_gated, me, slim)[...] = slot(send_gated, me, slim)[...]
    slot(got_back, n - 1 - me, slim)[...] = slot(send_back, me, slim)[...]
    pad_gated[pl.ds(0, n), :] = jnp.zeros((n, rows), f32)
    pad_back[pl.ds(0, n), :] = jnp.zeros((n, rows), f32)
    exchange_wait(forth_taps)
    exchange_wait(forth)

    lane = lax.broadcasted_iota(jnp.int32, (rows, rows), 1)
    line = lax.broadcasted_iota(jnp.int32, (rows, rows), 0)
    keep = lane >= line
    group = min(GROUP, n)

    def turned(source, c, index):
        row = source[pl.ds(index * slim + c, 1), :]
        return pltpu.roll(
            jnp.broadcast_to(row, (rows, rows)), 0, 1, stride=1, stride_axis=0
        )

    def channel(c, carry):
        pad_gated[pl.ds(n, n), :] = got_gated[pl.ds(c, n, stride=slim), :]
        pad_back[pl.ds(n, n), :] = got_back[pl.ds(c, n, stride=slim), :]

        def some_lags(q, total):
            matrices = []
            for source in (got_taps, got_gated):
                if isinstance(q, int):
                    before = jnp.zeros((rows, rows), f32)
                else:
                    before = turned(source, c, jnp.maximum(q * group - 1, 0))
                    before = jnp.where(q == 0, 0.0, before)
                parts = []
                for e in range(group):
                    now = turned(source, c, q * group + e)
                    parts.append(jnp.where(keep, now, before).astype(bf16))
                    before = now
                matrices.append(jnp.concatenate(parts, axis=0))
            table = jnp.concatenate(matrices, axis=1)
            lines = jnp.concatenate(
                [
                    jnp.concatenate(
                        [pad[pl.ds(n - q * group - e, n), :] for e in range(group)], axis=1
                    ).astype(bf16)
                    for pad in (pad_gated, pad_back)
                ],
                axis=0,
            )
            return total + jnp.dot(lines, table, preferred_element_type=f32)

        sums = jnp.zeros((2 * n, 2 * rows), f32)
        if n == group:
            sums = some_lags(0, sums)
        else:
            sums = lax.fori_loop(0, n // group, some_lags, sums)
        made_mixed[pl.ds(c, n, stride=slim), :] = sums[:n, :rows]
        late = reverse(jnp.concatenate([sums[n:, :rows], sums[n:, rows:]], axis=0))
        made_conv[pl.ds(c, n, stride=slim), :] = late[:n]
        made_taps[pl.ds(c, n, stride=slim), :] = late[n:]
        return carry

    lax.fori_loop(0, cpd, channel, 0)
    exchange_start(home)
    exchange_start(home_last)
    slot(home_mixed, me, slim)[...] = slot(made_mixed, me, slim)[...]
    slot(home_conv, me, slim)[...] = slot(made_conv, n - 1 - me, slim)[...]
    slot(home_taps, me, slim)[...] = slot(made_taps, n - 1 - me, slim)[...]

    def held(part, member):
        return slot(proj_all, part * TEAM + member, rows)

    def own(part):
        return proj.at[pl.ds(part * rows, rows), :]

    def direct(part, o, sender, peer):
        return remote(own(part), held(part, sender), send_sems.at[part, o],
                      recv_sems.at[part, sender], base + peer)

    def relay(part, o, member):
        return remote(held(part, member), held(part, member), relay_sems.at[part, o],
                      recv_sems.at[part, member], base + sibling)

    def across(o):
        return lax.rem(chip + o, CHIPS) * 2 + core

    def sums_copy(part, to_team, from_team, peer):
        return remote(slot(made, part * teams + to_team, block),
                      slot(got, part * teams + from_team, block),
                      send_sum_sems.at[part, to_team], recv_sum_sems.at[part, from_team],
                      peer * TEAM + mine)

    exchange_wait(home)
    conv = gather(home_conv).T * scaling
    mixed = gather(home_mixed).T * scaling
    values = (grad_ref[...].astype(f32) * mixed, conv * value_rows[...], conv * key_rows[...])
    for part in range(PARTS):
        rounded = values[part].astype(bf16).astype(f32)
        own(part)[...] = rounded
        held(part, mine)[...] = rounded
    for part in range(PARTS):
        for o in range(1, CHIPS):
            direct(part, o, mine, across(o)).start()
        direct(part, 0, mine, sibling).start()

    @pl.loop(1, TEAM)
    def _(o):
        other = lax.rem(mine + o, TEAM)
        cols(other, mine, other).wait_send()
        cols(other, other, other).wait_recv()

    for s in range(TEAM):
        left[:, s * rows : (s + 1) * rows] = got_cols[s * rows : (s + 1) * rows, :].T.astype(bf16)
    tile = min(512, depth)

    def grad_inputs_tiles(first, last):
        lines = jnp.concatenate(
            [own(part)[...].astype(bf16) for part in range(PARTS)], axis=1
        )

        @pl.loop(first, last)
        def _(t):
            start = pl.multiple_of(t * tile, tile)
            grad_inputs_ref[:, pl.ds(start, tile)] = lax.dot_general(
                lines, weights[pl.ds(start, tile), :], (((1,), (1,)), ((), ())),
                preferred_element_type=f32,
            ).astype(bf16)

    for part in range(PARTS):
        for o in range(1, CHIPS):
            direct(part, o, across(o), across(o)).wait_recv()
            relay(part, o, across(o)).start()
        direct(part, 0, sibling, sibling).wait_recv()
        for o in range(1, CHIPS):
            relay(part, o, lax.rem(chip + o, CHIPS) * 2 + 1 - core).wait_recv()
        right = proj_all[part * TEAM * rows : (part + 1) * TEAM * rows, :].astype(bf16)

        def product(index):
            lines = left[pl.ds(pl.multiple_of(index * block, 16), block), :]
            return jnp.dot(lines, right, preferred_element_type=f32)

        def send_one(o, carry):
            target = lax.rem(team + o, teams)
            slot(made, part * teams + target, block)[...] = product(target)
            sums_copy(part, target, team, target).start()
            return carry

        lax.fori_loop(1, teams, send_one, 0)
        out_ref[:, part * channels : (part + 1) * channels] = product(team)

    grad_inputs_tiles(0, depth // tile)
    exchange_wait(home_last)
    grad_taps_ref[...] = gather(home_taps).T * scaling

    for part in range(PARTS):
        span = slice(part * channels, (part + 1) * channels)

        def add_one(o, carry):
            other = lax.rem(team + o, teams)
            sums_copy(part, other, other, other).wait_recv()
            out_ref[:, span] = out_ref[:, span] + slot(got, part * teams + other, block)[...]
            return carry

        lax.fori_loop(1, teams, add_one, 0)
        out_ref[:, span] = out_ref[:, span] * scaling

    for plan in (forth_taps, forth, home, home_last):
        exchange_sent(plan)
    for part in range(PARTS):
        for o in range(1, CHIPS):
            direct(part, o, mine, across(o)).wait_send()
            relay(part, o, across(o)).wait_send()
        direct(part, 0, mine, sibling).wait_send()

        def sent_one(o, carry):
            target = lax.rem(team + o, teams)
            sums_copy(part, target, team, target).wait_send()
            return carry

        lax.fori_loop(1, teams, sent_one, 0)


def per_device(inputs, in_weight, filter_taps, grad_out):
    rows, depth = inputs.shape
    channels = filter_taps.shape[1]
    n = lax.axis_size("seq")
    scaling = 1.0 / math.sqrt(rows * n)
    slim = round_up(channels // n, 8)
    share = depth // TEAM
    f32, bf16 = jnp.float32, jnp.bfloat16
    vmem = pl.BlockSpec(memory_space=pltpu.VMEM)
    dma = pltpu.SemaphoreType.DMA
    return pl.pallas_call(
        functools.partial(fused_kernel, n, scaling),
        out_shape=(
            jax.ShapeDtypeStruct((rows, depth), bf16),
            jax.ShapeDtypeStruct((depth // n, PARTS * channels), f32),
            jax.ShapeDtypeStruct((rows, channels), f32),
        ),
        in_specs=[vmem, pl.BlockSpec(memory_space=pl.ANY), vmem, vmem],
        out_specs=(vmem,) * 3,
        scratch_shapes=[pltpu.VMEM((n * slim, rows), f32)] * 12
        + [
            pltpu.VMEM((2 * n, rows), f32),
            pltpu.VMEM((2 * n, rows), f32),
            pltpu.VMEM((TEAM * rows, share), f32),
            pltpu.VMEM((TEAM * rows, share), f32),
            pltpu.VMEM((share, TEAM * rows), bf16),
            pltpu.VMEM((rows, channels), f32),
            pltpu.VMEM((rows, channels), f32),
            pltpu.VMEM((PARTS * rows, channels), f32),
            pltpu.VMEM((PARTS * TEAM * rows, channels), f32),
            pltpu.VMEM((PARTS * share, channels), f32),
            pltpu.VMEM((PARTS * share, channels), f32),
            pltpu.VMEM(in_weight.shape, in_weight.dtype),
            dma((3, n)), dma((3, n)), dma((3, n)), dma((3, n)), dma((TEAM,)), dma((TEAM,)),
            dma((PARTS, CHIPS)), dma((PARTS, CHIPS)), dma((PARTS, TEAM)),
            dma((PARTS, n // TEAM)), dma((PARTS, n // TEAM)), dma((4,)),
        ],
        compiler_params=pltpu.CompilerParams(collective_id=0, has_side_effects=True),
    )(inputs, in_weight, filter_taps, grad_out)


def solution(mesh):
    in_specs = (P(("grp", "seq"), None), P(), P("seq", None), P(("grp", "seq"), None))
    out_specs = (P(("grp", "seq"), None), P(("grp", "seq"), None), P(("grp", "seq"), None))
    return jax.shard_map(
        per_device, mesh=mesh, in_specs=in_specs, out_specs=out_specs, check_vma=False
    )
```

```python
import functools
import math

import jax
import jax.numpy as jnp
from jax import lax
from jax.experimental import pallas as pl
from jax.experimental.pallas import tpu as pltpu
from jax.sharding import PartitionSpec as P

GROUP = 16
TEAM = 8
CHIPS = 4
PARTS = 6


def round_up(value, step):
    return (value + step - 1) // step * step


def remote(src, dst, send_sem, recv_sem, peer):
    return pltpu.make_async_remote_copy(
        src_ref=src,
        dst_ref=dst,
        send_sem=send_sem,
        recv_sem=recv_sem,
        device_id={"seq": peer},
        device_id_type=pl.DeviceIdType.MESH,
    )


def fused_kernel(
    n, scaling, x_ref, weight_ref, taps_ref, grad_ref,
    grad_inputs_ref, out_ref, grad_taps_ref,
    send_taps, send_gated, send_back, got_taps, got_gated, got_back,
    made_mixed, made_conv, made_taps, home_mixed, home_conv, home_taps,
    pad_gated, pad_back, send_cols, got_cols, left, key_rows, value_rows,
    proj, proj_all, made, got, weights,
    go_sems, come_sems, back_sems, home_sems, send_cols_sems, recv_cols_sems,
    send_sems, relay_sems, recv_sems, send_sum_sems, recv_sum_sems, weight_sems,
):
    f32, bf16 = jnp.float32, jnp.bfloat16
    me = lax.axis_index("seq")
    rows, depth = x_ref.shape
    channels = taps_ref.shape[1]
    width = 3 * channels // PARTS
    cpd = channels // n
    slim = send_taps.shape[0] // n
    teams = n // TEAM
    team, mine = me // TEAM, lax.rem(me, TEAM)
    base, chip, core = team * TEAM, mine // 2, lax.rem(mine, 2)
    sibling = chip * 2 + 1 - core
    block = depth // n
    share = depth // TEAM
    pieces = weight_sems.shape[0]
    piece = depth // pieces

    def slot(ref, index, height):
        return ref.at[pl.ds(pl.multiple_of(index * height, 8), height), :]

    def load(k):
        span = pl.ds(k * piece, piece)
        return pltpu.make_async_copy(
            weight_ref.at[span, :], weights.at[span, :], weight_sems.at[k]
        )

    for k in range(pieces):
        load(k).start()
    barrier = pltpu.get_barrier_semaphore()

    @pl.loop(1, n)
    def _(o):
        pl.semaphore_signal(
            barrier, inc=1, device_id={"seq": lax.rem(me + o, n)},
            device_id_type=pl.DeviceIdType.MESH,
        )

    def spread(ref, values):
        if slim == cpd:
            ref[...] = values
        else:
            for p in range(n):
                ref[p * slim : p * slim + cpd, :] = values[p * cpd : (p + 1) * cpd, :]

    def gather(ref):
        if slim == cpd:
            return ref[...]
        return jnp.concatenate([ref[p * slim : p * slim + cpd, :] for p in range(n)], axis=0)

    anti = (
        lax.broadcasted_iota(jnp.int32, (rows, rows), 0)
        + lax.broadcasted_iota(jnp.int32, (rows, rows), 1)
        == rows - 1
    ).astype(f32)

    def reverse(values):
        return jnp.dot(
            values, anti, preferred_element_type=f32, precision=lax.Precision.HIGHEST
        )

    spread(send_taps, taps_ref[...].T)
    for g in range(TEAM):
        for h in range(teams):
            first = (h * TEAM + g) * block
            send_cols[g * rows : (g + 1) * rows, h * block : (h + 1) * block] = x_ref[
                :, first : first + block
            ].astype(f32)
    pl.semaphore_wait(barrier, n - 1)

    def forth_taps(peer, sender):
        return (remote(slot(send_taps, peer, slim), slot(got_taps, sender, slim),
                       go_sems.at[0, peer], come_sems.at[0, sender], peer),)

    def forth(peer, sender):
        return (
            remote(slot(send_gated, peer, slim), slot(got_gated, sender, slim),
                   go_sems.at[1, peer], come_sems.at[1, sender], peer),
            remote(slot(send_back, peer, slim), slot(got_back, n - 1 - sender, slim),
                   go_sems.at[2, peer], come_sems.at[2, sender], peer),
        )

    def home(peer, sender):
        return (
            remote(slot(made_mixed, peer, slim), slot(home_mixed, sender, slim),
                   back_sems.at[0, peer], home_sems.at[0, sender], peer),
            remote(slot(made_conv, n - 1 - peer, slim), slot(home_conv, sender, slim),
                   back_sems.at[1, peer], home_sems.at[1, sender], peer),
        )

    def home_last(peer, sender):
        return (remote(slot(made_taps, n - 1 - peer, slim), slot(home_taps, sender, slim),
                       back_sems.at[2, peer], home_sems.at[2, sender], peer),)

    def exchange_start(plan):
        @pl.loop(1, n)
        def _(o):
            for copy in plan(lax.rem(me + o, n), me):
                copy.start()

    def exchange_wait(plan):
        @pl.loop(1, n)
        def _(o):
            other = lax.rem(me + n - o, n)
            for copy in plan(other, other):
                copy.wait_recv()

    def exchange_sent(plan):
        @pl.loop(1, n)
        def _(o):
            for copy in plan(lax.rem(me + o, n), me):
                copy.wait_send()

    def cols(target, sender, peer):
        return remote(slot(send_cols, target, rows), slot(got_cols, sender, rows),
                      send_cols_sems.at[target], recv_cols_sems.at[sender], base + peer)

    def cols_start(other):
        cols(other, mine, other).start()

    exchange_start(forth_taps)
    near = (chip + 1 - 2 * lax.rem(chip, 2)) * 2
    next_pair = lax.rem(chip + 2, CHIPS) * 2
    corner = lax.rem(chip + 3 - 2 * lax.rem(chip, 2), CHIPS) * 2
    cols_start(sibling)
    cols_start(near + core)
    cols_start(next_pair + core)
    total = jnp.zeros((rows, 3 * channels), f32)
    for k in range(pieces):
        load(k).wait()
        total = total + jnp.dot(
            x_ref[:, k * piece : (k + 1) * piece], weights[k * piece : (k + 1) * piece, :],
            preferred_element_type=f32,
        )
    total = total.astype(bf16).astype(f32)
    key_rows[...] = total[:, channels : 2 * channels]
    value_rows[...] = total[:, 2 * channels :]
    spread(send_gated, (total[:, channels : 2 * channels] * total[:, 2 * channels :]).T)
    spread(send_back, reverse((grad_ref[...].astype(f32) * total[:, :channels]).T))
    exchange_start(forth)
    cols_start(near + 1 - core)
    cols_start(next_pair + 1 - core)
    cols_start(corner + core)
    cols_start(corner + 1 - core)

    slot(got_cols, mine, rows)[...] = slot(send_cols, mine, rows)[...]
    slot(got_taps, me, slim)[...] = slot(send_taps, me, slim)[...]
    slot(got_gated, me, slim)[...] = slot(send_gated, me, slim)[...]
    slot(got_back, n - 1 - me, slim)[...] = slot(send_back, me, slim)[...]
    pad_gated[pl.ds(0, n), :] = jnp.zeros((n, rows), f32)
    pad_back[pl.ds(0, n), :] = jnp.zeros((n, rows), f32)
    exchange_wait(forth_taps)
    exchange_wait(forth)

    lane = lax.broadcasted_iota(jnp.int32, (rows, rows), 1)
    line = lax.broadcasted_iota(jnp.int32, (rows, rows), 0)
    keep = lane >= line
    group = min(GROUP, n)

    def turned(source, c, index):
        row = source[pl.ds(index * slim + c, 1), :]
        return pltpu.roll(
            jnp.broadcast_to(row, (rows, rows)), 0, 1, stride=1, stride_axis=0
        )

    def channel(c, carry):
        pad_gated[pl.ds(n, n), :] = got_gated[pl.ds(c, n, stride=slim), :]
        pad_back[pl.ds(n, n), :] = got_back[pl.ds(c, n, stride=slim), :]

        def some_lags(q, total):
            matrices = []
            for source in (got_taps, got_gated):
                if isinstance(q, int):
                    before = jnp.zeros((rows, rows), f32)
                else:
                    before = turned(source, c, jnp.maximum(q * group - 1, 0))
                    before = jnp.where(q == 0, 0.0, before)
                parts = []
                for e in range(group):
                    now = turned(source, c, q * group + e)
                    parts.append(jnp.where(keep, now, before).astype(bf16))
                    before = now
                matrices.append(jnp.concatenate(parts, axis=0))
            table = jnp.concatenate(matrices, axis=1)
            lines = jnp.concatenate(
                [
                    jnp.concatenate(
                        [pad[pl.ds(n - q * group - e, n), :] for e in range(group)], axis=1
                    ).astype(bf16)
                    for pad in (pad_gated, pad_back)
                ],
                axis=0,
            )
            return total + jnp.dot(lines, table, preferred_element_type=f32)

        sums = jnp.zeros((2 * n, 2 * rows), f32)
        if n == group:
            sums = some_lags(0, sums)
        else:
            sums = lax.fori_loop(0, n // group, some_lags, sums)
        made_mixed[pl.ds(c, n, stride=slim), :] = sums[:n, :rows]
        late = reverse(jnp.concatenate([sums[n:, :rows], sums[n:, rows:]], axis=0))
        made_conv[pl.ds(c, n, stride=slim), :] = late[:n]
        made_taps[pl.ds(c, n, stride=slim), :] = late[n:]
        return carry

    lax.fori_loop(0, cpd, channel, 0)
    exchange_start(home)
    slot(home_mixed, me, slim)[...] = slot(made_mixed, me, slim)[...]
    slot(home_conv, me, slim)[...] = slot(made_conv, n - 1 - me, slim)[...]
    slot(home_taps, me, slim)[...] = slot(made_taps, n - 1 - me, slim)[...]

    def held(part, member):
        return slot(proj_all, part * TEAM + member, rows)

    def own(part):
        return proj.at[pl.ds(part * rows, rows), :]

    def direct(part, o, sender, peer):
        return remote(own(part), held(part, sender), send_sems.at[part, o],
                      recv_sems.at[part, sender], base + peer)

    def relay(part, o, member):
        return remote(held(part, member), held(part, member), relay_sems.at[part, o],
                      recv_sems.at[part, member], base + sibling)

    def across(o):
        return lax.rem(chip + o, CHIPS) * 2 + core

    def sums_copy(part, to_team, from_team, peer):
        return remote(slot(made, part * teams + to_team, block),
                      slot(got, part * teams + from_team, block),
                      send_sum_sems.at[part, to_team], recv_sum_sems.at[part, from_team],
                      peer * TEAM + mine)

    exchange_wait(home)
    conv = gather(home_conv).T * scaling
    mixed = gather(home_mixed).T * scaling
    values = jnp.concatenate(
        [grad_ref[...].astype(f32) * mixed, conv * value_rows[...], conv * key_rows[...]], axis=1
    )
    for part in range(PARTS):
        rounded = values[:, part * width : (part + 1) * width].astype(bf16).astype(f32)
        own(part)[...] = rounded
        held(part, mine)[...] = rounded
    for part in range(PARTS):
        for o in range(1, CHIPS):
            direct(part, o, mine, across(o)).start()
        direct(part, 0, mine, sibling).start()
    exchange_start(home_last)

    @pl.loop(1, TEAM)
    def _(o):
        other = lax.rem(mine + o, TEAM)
        cols(other, mine, other).wait_send()
        cols(other, other, other).wait_recv()

    for s in range(TEAM):
        left[:, s * rows : (s + 1) * rows] = got_cols[s * rows : (s + 1) * rows, :].T.astype(bf16)
    tile = min(512, depth)

    def grad_inputs_tiles(first, last):
        lines = jnp.concatenate(
            [own(part)[...].astype(bf16) for part in range(PARTS)], axis=1
        )

        @pl.loop(first, last)
        def _(t):
            start = pl.multiple_of(t * tile, tile)
            grad_inputs_ref[:, pl.ds(start, tile)] = lax.dot_general(
                lines, weights[pl.ds(start, tile), :], (((1,), (1,)), ((), ())),
                preferred_element_type=f32,
            ).astype(bf16)

    for part in range(PARTS):
        for o in range(1, CHIPS):
            direct(part, o, across(o), across(o)).wait_recv()
            relay(part, o, across(o)).start()
        direct(part, 0, sibling, sibling).wait_recv()
        for o in range(1, CHIPS):
            relay(part, o, lax.rem(chip + o, CHIPS) * 2 + 1 - core).wait_recv()
        right = proj_all[part * TEAM * rows : (part + 1) * TEAM * rows, :].astype(bf16)

        def product(index):
            lines = left[pl.ds(pl.multiple_of(index * block, 16), block), :]
            return jnp.dot(lines, right, preferred_element_type=f32)

        def send_one(o, carry):
            target = lax.rem(team + o, teams)
            slot(made, part * teams + target, block)[...] = product(target)
            sums_copy(part, target, team, target).start()
            return carry

        lax.fori_loop(1, teams, send_one, 0)
        out_ref[:, part * width : (part + 1) * width] = product(team)

    grad_inputs_tiles(0, depth // tile)
    exchange_wait(home_last)
    grad_taps_ref[...] = gather(home_taps).T * scaling

    for part in range(PARTS):
        span = slice(part * width, (part + 1) * width)

        def add_one(o, carry):
            other = lax.rem(team + o, teams)
            sums_copy(part, other, other, other).wait_recv()
            out_ref[:, span] = out_ref[:, span] + slot(got, part * teams + other, block)[...]
            return carry

        lax.fori_loop(1, teams, add_one, 0)
        out_ref[:, span] = out_ref[:, span] * scaling

    for plan in (forth_taps, forth, home, home_last):
        exchange_sent(plan)
    for part in range(PARTS):
        for o in range(1, CHIPS):
            direct(part, o, mine, across(o)).wait_send()
            relay(part, o, across(o)).wait_send()
        direct(part, 0, mine, sibling).wait_send()

        def sent_one(o, carry):
            target = lax.rem(team + o, teams)
            sums_copy(part, target, team, target).wait_send()
            return carry

        lax.fori_loop(1, teams, sent_one, 0)


def write_kernel(*refs):
    sems = refs[-1]
    copies = [pltpu.make_async_copy(refs[k], refs[3 + k], sems.at[k]) for k in range(3)]
    for copy in copies:
        copy.start()
    for copy in copies:
        copy.wait()


def per_device(inputs, in_weight, filter_taps, grad_out):
    rows, depth = inputs.shape
    channels = filter_taps.shape[1]
    n = lax.axis_size("seq")
    scaling = 1.0 / math.sqrt(rows * n)
    slim = round_up(channels // n, 8)
    share = depth // TEAM
    width = 3 * channels // PARTS
    f32, bf16 = jnp.float32, jnp.bfloat16
    vmem = pl.BlockSpec(memory_space=pltpu.VMEM)
    dma = pltpu.SemaphoreType.DMA
    results = pl.pallas_call(
        functools.partial(fused_kernel, n, scaling),
        out_shape=(
            jax.ShapeDtypeStruct((rows, depth), bf16),
            jax.ShapeDtypeStruct((depth // n, 3 * channels), f32),
            jax.ShapeDtypeStruct((rows, channels), f32),
        ),
        in_specs=[vmem, pl.BlockSpec(memory_space=pl.ANY), vmem, vmem],
        out_specs=(vmem,) * 3,
        scratch_shapes=[pltpu.VMEM((n * slim, rows), f32)] * 12
        + [
            pltpu.VMEM((2 * n, rows), f32),
            pltpu.VMEM((2 * n, rows), f32),
            pltpu.VMEM((TEAM * rows, share), f32),
            pltpu.VMEM((TEAM * rows, share), f32),
            pltpu.VMEM((share, TEAM * rows), bf16),
            pltpu.VMEM((rows, channels), f32),
            pltpu.VMEM((rows, channels), f32),
            pltpu.VMEM((PARTS * rows, width), f32),
            pltpu.VMEM((PARTS * TEAM * rows, width), f32),
            pltpu.VMEM((PARTS * share, width), f32),
            pltpu.VMEM((PARTS * share, width), f32),
            pltpu.VMEM(in_weight.shape, in_weight.dtype),
            dma((3, n)), dma((3, n)), dma((3, n)), dma((3, n)), dma((TEAM,)), dma((TEAM,)),
            dma((PARTS, CHIPS)), dma((PARTS, CHIPS)), dma((PARTS, TEAM)),
            dma((PARTS, n // TEAM)), dma((PARTS, n // TEAM)), dma((4,)),
        ],
        compiler_params=pltpu.CompilerParams(
            collective_id=0, has_side_effects=True, vmem_limit_bytes=59 << 20
        ),
    )(inputs, in_weight, filter_taps, grad_out)
    return pl.pallas_call(
        write_kernel,
        out_shape=tuple(jax.ShapeDtypeStruct(r.shape, r.dtype) for r in results),
        in_specs=[vmem] * 3,
        out_specs=(pl.BlockSpec(memory_space=pl.ANY),) * 3,
        scratch_shapes=[dma((3,))],
        compiler_params=pltpu.CompilerParams(vmem_limit_bytes=8 << 20),
    )(*results)


def solution(mesh):
    in_specs = (P(("grp", "seq"), None), P(), P("seq", None), P(("grp", "seq"), None))
    out_specs = (P(("grp", "seq"), None), P(("grp", "seq"), None), P(("grp", "seq"), None))
    return jax.shard_map(
        per_device, mesh=mesh, in_specs=in_specs, out_specs=out_specs, check_vma=False
    )
```

```python
import functools
import math

import jax
import jax.numpy as jnp
from jax import lax
from jax.experimental import pallas as pl
from jax.experimental.pallas import tpu as pltpu
from jax.sharding import PartitionSpec as P

GROUP = 16
TEAM = 8
CHIPS = 4
PARTS = 6


def round_up(value, step):
    return (value + step - 1) // step * step


def remote(src, dst, send_sem, recv_sem, peer):
    return pltpu.make_async_remote_copy(
        src_ref=src,
        dst_ref=dst,
        send_sem=send_sem,
        recv_sem=recv_sem,
        device_id={"seq": peer},
        device_id_type=pl.DeviceIdType.MESH,
    )


def fused_kernel(
    n, scaling, x_ref, weight_ref, taps_ref, grad_ref,
    grad_inputs_ref, out_ref, grad_taps_ref,
    send_taps, send_gated, send_back, got_taps, got_gated, got_back,
    made_mixed, made_conv, made_taps, home_mixed, home_conv, home_taps,
    pad_gated, pad_back, send_cols, got_cols, left, key_rows, value_rows,
    proj, proj_all, made, got, weights,
    go_sems, come_sems, back_sems, home_sems, send_cols_sems, recv_cols_sems,
    send_sems, relay_sems, recv_sems, send_sum_sems, recv_sum_sems, weight_sems,
):
    f32, bf16 = jnp.float32, jnp.bfloat16
    me = lax.axis_index("seq")
    rows, depth = x_ref.shape
    channels = taps_ref.shape[1]
    width = 3 * channels // PARTS
    cpd = channels // n
    slim = send_taps.shape[0] // n
    teams = n // TEAM
    team, mine = me // TEAM, lax.rem(me, TEAM)
    base, chip, core = team * TEAM, mine // 2, lax.rem(mine, 2)
    sibling = chip * 2 + 1 - core
    block = depth // n
    share = depth // TEAM
    pieces = weight_sems.shape[0]
    piece = depth // pieces

    def slot(ref, index, height):
        return ref.at[pl.ds(pl.multiple_of(index * height, 8), height), :]

    def load(k):
        span = pl.ds(k * piece, piece)
        return pltpu.make_async_copy(
            weight_ref.at[span, :], weights.at[span, :], weight_sems.at[k]
        )

    for k in range(pieces):
        load(k).start()
    barrier = pltpu.get_barrier_semaphore()

    @pl.loop(1, n)
    def _(o):
        pl.semaphore_signal(
            barrier, inc=1, device_id={"seq": lax.rem(me + o, n)},
            device_id_type=pl.DeviceIdType.MESH,
        )

    def spread(ref, values):
        if slim == cpd:
            ref[...] = values
        else:
            for p in range(n):
                ref[p * slim : p * slim + cpd, :] = values[p * cpd : (p + 1) * cpd, :]

    def gather(ref):
        if slim == cpd:
            return ref[...]
        return jnp.concatenate([ref[p * slim : p * slim + cpd, :] for p in range(n)], axis=0)

    anti = (
        lax.broadcasted_iota(jnp.int32, (rows, rows), 0)
        + lax.broadcasted_iota(jnp.int32, (rows, rows), 1)
        == rows - 1
    ).astype(f32)

    def reverse(values):
        return jnp.dot(
            values, anti, preferred_element_type=f32, precision=lax.Precision.HIGHEST
        )

    spread(send_taps, taps_ref[...].T)
    for g in range(TEAM):
        for h in range(teams):
            first = (h * TEAM + g) * block
            send_cols[g * rows : (g + 1) * rows, h * block : (h + 1) * block] = x_ref[
                :, first : first + block
            ].astype(f32)
    pl.semaphore_wait(barrier, n - 1)

    def forth_taps(peer, sender):
        return (remote(slot(send_taps, peer, slim), slot(got_taps, sender, slim),
                       go_sems.at[0, peer], come_sems.at[0, sender], peer),)

    def forth(peer, sender):
        return (
            remote(slot(send_gated, peer, slim), slot(got_gated, sender, slim),
                   go_sems.at[1, peer], come_sems.at[1, sender], peer),
            remote(slot(send_back, peer, slim), slot(got_back, n - 1 - sender, slim),
                   go_sems.at[2, peer], come_sems.at[2, sender], peer),
        )

    def home(peer, sender):
        return (
            remote(slot(made_mixed, peer, slim), slot(home_mixed, sender, slim),
                   back_sems.at[0, peer], home_sems.at[0, sender], peer),
            remote(slot(made_conv, n - 1 - peer, slim), slot(home_conv, sender, slim),
                   back_sems.at[1, peer], home_sems.at[1, sender], peer),
        )

    def home_last(peer, sender):
        return (remote(slot(made_taps, n - 1 - peer, slim), slot(home_taps, sender, slim),
                       back_sems.at[2, peer], home_sems.at[2, sender], peer),)

    def exchange_start(plan):
        @pl.loop(1, n)
        def _(o):
            for copy in plan(lax.rem(me + o, n), me):
                copy.start()

    def exchange_wait(plan):
        @pl.loop(1, n)
        def _(o):
            other = lax.rem(me + n - o, n)
            for copy in plan(other, other):
                copy.wait_recv()

    def exchange_sent(plan):
        @pl.loop(1, n)
        def _(o):
            for copy in plan(lax.rem(me + o, n), me):
                copy.wait_send()

    def cols(target, sender, peer):
        return remote(slot(send_cols, target, rows), slot(got_cols, sender, rows),
                      send_cols_sems.at[target], recv_cols_sems.at[sender], base + peer)

    def cols_start(other):
        cols(other, mine, other).start()

    exchange_start(forth_taps)
    near = (chip + 1 - 2 * lax.rem(chip, 2)) * 2
    next_pair = lax.rem(chip + 2, CHIPS) * 2
    corner = lax.rem(chip + 3 - 2 * lax.rem(chip, 2), CHIPS) * 2
    cols_start(sibling)
    cols_start(near + core)
    cols_start(next_pair + core)
    total = jnp.zeros((rows, 3 * channels), f32)
    for k in range(pieces):
        load(k).wait()
        total = total + jnp.dot(
            x_ref[:, k * piece : (k + 1) * piece], weights[k * piece : (k + 1) * piece, :],
            preferred_element_type=f32,
        )
    total = total.astype(bf16).astype(f32)
    key_rows[...] = total[:, channels : 2 * channels]
    value_rows[...] = total[:, 2 * channels :]
    spread(send_gated, (total[:, channels : 2 * channels] * total[:, 2 * channels :]).T)
    spread(send_back, reverse((grad_ref[...].astype(f32) * total[:, :channels]).T))
    exchange_start(forth)
    cols_start(near + 1 - core)
    cols_start(next_pair + 1 - core)
    cols_start(corner + core)
    cols_start(corner + 1 - core)

    slot(got_cols, mine, rows)[...] = slot(send_cols, mine, rows)[...]
    slot(got_taps, me, slim)[...] = slot(send_taps, me, slim)[...]
    slot(got_gated, me, slim)[...] = slot(send_gated, me, slim)[...]
    slot(got_back, n - 1 - me, slim)[...] = slot(send_back, me, slim)[...]
    pad_gated[pl.ds(0, n), :] = jnp.zeros((n, rows), f32)
    pad_back[pl.ds(0, n), :] = jnp.zeros((n, rows), f32)
    exchange_wait(forth_taps)
    exchange_wait(forth)

    lane = lax.broadcasted_iota(jnp.int32, (rows, rows), 1)
    line = lax.broadcasted_iota(jnp.int32, (rows, rows), 0)
    keep = lane >= line
    group = min(GROUP, n)

    def turned(source, c, index):
        row = source[pl.ds(index * slim + c, 1), :]
        return pltpu.roll(
            jnp.broadcast_to(row, (rows, rows)), 0, 1, stride=1, stride_axis=0
        )

    def channel(c, carry):
        pad_gated[pl.ds(n, n), :] = got_gated[pl.ds(c, n, stride=slim), :]
        pad_back[pl.ds(n, n), :] = got_back[pl.ds(c, n, stride=slim), :]

        def some_lags(q, total):
            matrices = []
            for source in (got_taps, got_gated):
                if isinstance(q, int):
                    before = jnp.zeros((rows, rows), f32)
                else:
                    before = turned(source, c, jnp.maximum(q * group - 1, 0))
                    before = jnp.where(q == 0, 0.0, before)
                parts = []
                for e in range(group):
                    now = turned(source, c, q * group + e)
                    parts.append(jnp.where(keep, now, before).astype(bf16))
                    before = now
                matrices.append(jnp.concatenate(parts, axis=0))
            table = jnp.concatenate(matrices, axis=1)
            lines = jnp.concatenate(
                [
                    jnp.concatenate(
                        [pad[pl.ds(n - q * group - e, n), :] for e in range(group)], axis=1
                    ).astype(bf16)
                    for pad in (pad_gated, pad_back)
                ],
                axis=0,
            )
            return total + jnp.dot(lines, table, preferred_element_type=f32)

        sums = jnp.zeros((2 * n, 2 * rows), f32)
        if n == group:
            sums = some_lags(0, sums)
        else:
            sums = lax.fori_loop(0, n // group, some_lags, sums)
        made_mixed[pl.ds(c, n, stride=slim), :] = sums[:n, :rows]
        late = reverse(jnp.concatenate([sums[n:, :rows], sums[n:, rows:]], axis=0))
        made_conv[pl.ds(c, n, stride=slim), :] = late[:n]
        made_taps[pl.ds(c, n, stride=slim), :] = late[n:]
        return carry

    lax.fori_loop(0, cpd, channel, 0)
    exchange_start(home)
    slot(home_mixed, me, slim)[...] = slot(made_mixed, me, slim)[...]
    slot(home_conv, me, slim)[...] = slot(made_conv, n - 1 - me, slim)[...]
    slot(home_taps, me, slim)[...] = slot(made_taps, n - 1 - me, slim)[...]

    def held(part, member):
        return slot(proj_all, part * TEAM + member, rows)

    def own(part):
        return proj.at[pl.ds(part * rows, rows), :]

    def direct(part, o, sender, peer):
        return remote(own(part), held(part, sender), send_sems.at[part, o],
                      recv_sems.at[part, sender], base + peer)

    def relay(part, o, member):
        return remote(held(part, member), held(part, member), relay_sems.at[part, o],
                      recv_sems.at[part, member], base + sibling)

    def across(o):
        return lax.rem(chip + o, CHIPS) * 2 + core

    def sums_copy(part, to_team, from_team, peer):
        return remote(slot(made, part * teams + to_team, block),
                      slot(got, part * teams + from_team, block),
                      send_sum_sems.at[part, to_team], recv_sum_sems.at[part, from_team],
                      peer * TEAM + mine)

    exchange_wait(home)
    conv = gather(home_conv).T * scaling
    mixed = gather(home_mixed).T * scaling
    values = jnp.concatenate(
        [grad_ref[...].astype(f32) * mixed, conv * value_rows[...], conv * key_rows[...]], axis=1
    )
    for part in range(PARTS):
        rounded = values[:, part * width : (part + 1) * width].astype(bf16).astype(f32)
        own(part)[...] = rounded
        held(part, mine)[...] = rounded
    for part in range(PARTS):
        for o in range(1, CHIPS):
            direct(part, o, mine, across(o)).start()
        direct(part, 0, mine, sibling).start()
    exchange_start(home_last)

    @pl.loop(1, TEAM)
    def _(o):
        other = lax.rem(mine + o, TEAM)
        cols(other, mine, other).wait_send()
        cols(other, other, other).wait_recv()

    for s in range(TEAM):
        left[:, s * rows : (s + 1) * rows] = got_cols[s * rows : (s + 1) * rows, :].T.astype(bf16)
    tile = min(512, depth)

    def grad_inputs_tiles(first, last):
        lines = jnp.concatenate(
            [own(part)[...].astype(bf16) for part in range(PARTS)], axis=1
        )

        @pl.loop(first, last)
        def _(t):
            start = pl.multiple_of(t * tile, tile)
            grad_inputs_ref[:, pl.ds(start, tile)] = lax.dot_general(
                lines, weights[pl.ds(start, tile), :], (((1,), (1,)), ((), ())),
                preferred_element_type=f32,
            ).astype(bf16)

    for part in range(PARTS):
        for o in range(1, CHIPS):
            direct(part, o, across(o), across(o)).wait_recv()
            relay(part, o, across(o)).start()
        direct(part, 0, sibling, sibling).wait_recv()
        for o in range(1, CHIPS):
            relay(part, o, lax.rem(chip + o, CHIPS) * 2 + 1 - core).wait_recv()
        right = proj_all[part * TEAM * rows : (part + 1) * TEAM * rows, :].astype(bf16)

        def product(index):
            lines = left[pl.ds(pl.multiple_of(index * block, 16), block), :]
            return jnp.dot(lines, right, preferred_element_type=f32)

        def send_one(o, carry):
            target = lax.rem(team + o, teams)
            slot(made, part * teams + target, block)[...] = product(target)
            sums_copy(part, target, team, target).start()
            return carry

        lax.fori_loop(1, teams, send_one, 0)
        out_ref[:, part * width : (part + 1) * width] = product(team)

    grad_inputs_tiles(0, depth // tile)
    exchange_wait(home_last)
    grad_taps_ref[...] = gather(home_taps).T * scaling

    for part in range(PARTS):
        span = slice(part * width, (part + 1) * width)

        def add_one(o, carry):
            other = lax.rem(team + o, teams)
            sums_copy(part, other, other, other).wait_recv()
            out_ref[:, span] = out_ref[:, span] + slot(got, part * teams + other, block)[...]
            return carry

        lax.fori_loop(1, teams, add_one, 0)
        out_ref[:, span] = out_ref[:, span] * scaling

    for plan in (forth_taps, forth, home, home_last):
        exchange_sent(plan)
    for part in range(PARTS):
        for o in range(1, CHIPS):
            direct(part, o, mine, across(o)).wait_send()
            relay(part, o, across(o)).wait_send()
        direct(part, 0, mine, sibling).wait_send()

        def sent_one(o, carry):
            target = lax.rem(team + o, teams)
            sums_copy(part, target, team, target).wait_send()
            return carry

        lax.fori_loop(1, teams, sent_one, 0)


def write_kernel(*refs):
    sems = refs[-1]
    copies = [pltpu.make_async_copy(refs[k], refs[3 + k], sems.at[k]) for k in range(3)]
    for copy in copies:
        copy.start()
    for copy in copies:
        copy.wait()


def per_device(inputs, in_weight, filter_taps, grad_out):
    rows, depth = inputs.shape
    channels = filter_taps.shape[1]
    n = lax.axis_size("seq")
    scaling = 1.0 / math.sqrt(rows * n)
    slim = round_up(channels // n, 8)
    share = depth // TEAM
    width = 3 * channels // PARTS
    f32, bf16 = jnp.float32, jnp.bfloat16
    vmem = pl.BlockSpec(memory_space=pltpu.VMEM)
    dma = pltpu.SemaphoreType.DMA
    results = pl.pallas_call(
        functools.partial(fused_kernel, n, scaling),
        out_shape=(
            jax.ShapeDtypeStruct((rows, depth), bf16),
            jax.ShapeDtypeStruct((depth // n, 3 * channels), f32),
            jax.ShapeDtypeStruct((rows, channels), f32),
        ),
        in_specs=[vmem, pl.BlockSpec(memory_space=pl.ANY), vmem, vmem],
        out_specs=(vmem,) * 3,
        scratch_shapes=[pltpu.VMEM((n * slim, rows), f32)] * 12
        + [
            pltpu.VMEM((2 * n, rows), f32),
            pltpu.VMEM((2 * n, rows), f32),
            pltpu.VMEM((TEAM * rows, share), f32),
            pltpu.VMEM((TEAM * rows, share), f32),
            pltpu.VMEM((share, TEAM * rows), bf16),
            pltpu.VMEM((rows, channels), f32),
            pltpu.VMEM((rows, channels), f32),
            pltpu.VMEM((PARTS * rows, width), f32),
            pltpu.VMEM((PARTS * TEAM * rows, width), f32),
            pltpu.VMEM((PARTS * share, width), f32),
            pltpu.VMEM((PARTS * share, width), f32),
            pltpu.VMEM(in_weight.shape, in_weight.dtype),
            dma((3, n)), dma((3, n)), dma((3, n)), dma((3, n)), dma((TEAM,)), dma((TEAM,)),
            dma((PARTS, CHIPS)), dma((PARTS, CHIPS)), dma((PARTS, TEAM)),
            dma((PARTS, n // TEAM)), dma((PARTS, n // TEAM)), dma((4,)),
        ],
        compiler_params=pltpu.CompilerParams(
            collective_id=0, has_side_effects=True, vmem_limit_bytes=44 << 20
        ),
    )(inputs, in_weight, filter_taps, grad_out)
    return pl.pallas_call(
        write_kernel,
        out_shape=tuple(jax.ShapeDtypeStruct(r.shape, r.dtype) for r in results),
        in_specs=[vmem] * 3,
        out_specs=(pl.BlockSpec(memory_space=pl.ANY),) * 3,
        scratch_shapes=[dma((3,))],
        compiler_params=pltpu.CompilerParams(vmem_limit_bytes=8 << 20),
    )(*results)


def solution(mesh):
    in_specs = (P(("grp", "seq"), None), P(), P("seq", None), P(("grp", "seq"), None))
    out_specs = (P(("grp", "seq"), None), P(("grp", "seq"), None), P(("grp", "seq"), None))
    return jax.shard_map(
        per_device, mesh=mesh, in_specs=in_specs, out_specs=out_specs, check_vma=False
    )
```
